32 devices in a mesh: wide: 16 (over z, x, core), narrow: 2 (over y).
Axes of the slice: x: 2, y: 2, z: 4, core: 2. Of those that a mesh axis runs over, the one named last changes fastest.
Arguments:
- hidden_in: bfloat16 [2, 32, 256, 1024], P(None, ('wide', 'narrow')), may hold values from -6 to 6
- segment_ids: int32 [2, 32, 256], P(None, ('wide', 'narrow')), may hold values from 0 to 7, never falling along the last dimension, each value on 1 to 96 neighbouring positions
- rel_bucket: int32 [2, 32, 256, 256], P(None, ('wide', 'narrow')), may hold values from 0 to 31
- layout_bucket: int32 [2, 32, 256, 256], P(None, ('wide', 'narrow')), may hold values from 0 to 63
- w_query: bfloat16 [1024, 1024], P(('wide', 'narrow')), may hold values from -0.078125 to 0.078125
- w_key: bfloat16 [1024, 1024], P(('wide', 'narrow')), may hold values from -0.078125 to 0.078125
- w_value: bfloat16 [1024, 1024], P(('wide', 'narrow')), may hold values from -0.1875 to 0.1875
- w_out: bfloat16 [1024, 1024], P(('wide', 'narrow')), may hold values from -0.75 to 0.75
- norm_one: bfloat16 [1024], P(('wide', 'narrow')), may hold values from 0.5 to 1.5
- rel_table: bfloat16 [512], P(('wide', 'narrow')), may hold values from -3 to 3
- layout_table: bfloat16 [1024], P(('wide', 'narrow')), may hold values from -3 to 3
- norm_two: bfloat16 [1024], P(('wide', 'narrow')), may hold values from 0.5 to 1.5
- w_gate: bfloat16 [1024, 2816], P(('wide', 'narrow')), may hold values from -0.1875 to 0.1875
- w_up: bfloat16 [1024, 2816], P(('wide', 'narrow')), may hold values from -0.1875 to 0.1875
- w_down: bfloat16 [2816, 1024], P(('wide', 'narrow')), may hold values from -0.15625 to 0.15625
- out_grad: bfloat16 [2, 32, 256, 1024], P(None, ('wide', 'narrow')), may hold values from -6 to 6
Outputs:
- output: bfloat16 [2, 32, 256, 1024], P(None, ('wide', 'narrow'))
- in_grad: bfloat16 [2, 32, 256, 1024], P(None, ('wide', 'narrow'))
- grad_w_query: float32 [1024, 1024], P(('wide', 'narrow'))
- grad_w_key: float32 [1024, 1024], P(('wide', 'narrow'))
- grad_w_value: float32 [1024, 1024], P(('wide', 'narrow'))
- grad_w_out: float32 [1024, 1024], P(('wide', 'narrow'))
- grad_norm_one: float32 [1024], P(('wide', 'narrow'))
- grad_rel_table: float32 [512], P(('wide', 'narrow'))
- grad_layout_table: float32 [1024], P(('wide', 'narrow'))
- grad_norm_two: float32 [1024], P(('wide', 'narrow'))
- grad_w_gate: float32 [1024, 2816], P(('wide', 'narrow'))
- grad_w_up: float32 [1024, 2816], P(('wide', 'narrow'))
- grad_w_down: float32 [2816, 1024], P(('wide', 'narrow'))
The draws below stay inside these ranges and needn't reach their ends.
All inputs are finite; a program needn't handle non-finite values.
Results may differ from the reference program's by a relative error of at most 0.017.
Values may be sent and summed in bfloat16 or wider, within the bound.
A program may use at most 192 MiB of HBM per device.

```python
import math
import jax
import jax.numpy as jnp
import numpy as np
from jax import lax

D = 1024
HEADS = 16
HEAD_DIM = 64
FF = 2816
REL_BUCKETS = 32
LAYOUT_BUCKETS = 64
SEQ_LEN = 256
SEGS = 8
SEG_MOST = 96
MB = 2
INNER = 1024
SEQS = 32


def touch_ends(array, key, low, high):
    dims = array.shape
    index_at = [jax.random.randint(jax.random.fold_in(key, axis), (), 0, dims[axis]) for axis in range(len(dims))]
    array = array.at[tuple(index_at)].set(low)
    longest = dims.index(max(dims))
    index_at[longest] = (index_at[longest] + 1) % dims[longest]
    return array.at[tuple(index_at)].set(high)


def steps_of(key, dims, pieces, low, top_value):
    level = 1.0
    for dim, parts in pieces:
        draws = jax.random.uniform(jax.random.fold_in(jax.random.fold_in(key, 6), dim), (parts,), jnp.float32, low / len(pieces), top_value / len(pieces))
        level = level * jnp.repeat(jnp.exp(draws), dims[dim] // parts).reshape((-1,) + (1,) * (len(dims) - 1 - dim))
    return level


def split_up(amount, total, bound, slope):
    loads = [(1 << 20) // math.isqrt(rank ** slope) + 1 for rank in range(2, amount + 1)]
    rest, counts = total - bound - (amount - 1), [1] * (amount - 1)
    while rest > 0:
        free = [i for i in range(amount - 1) if counts[i] < bound]
        whole, budget = sum([loads[i] for i in free]), rest
        for i in free:
            extra = min(bound - counts[i], max(1, budget * loads[i] // whole), rest)
            counts[i] = counts[i] + extra
            rest = rest - extra
    return np.array([bound] + counts)


def uneven_parts(key, number_of, total, bound, lean):
    if number_of == 2:
        one = jax.random.randint(key, (), max(1, total - bound), min(bound, total - 1) + 1)
        return jnp.stack([one, total - one])
    lengths = jnp.asarray(split_up(number_of, total, bound, lean), jnp.int32)
    pairs = (number_of - 1) // 2
    donor, taker = lengths[1:1 + 2 * pairs:2], lengths[2:2 + 2 * pairs:2]
    room = jnp.minimum(donor - 1, bound - taker)
    passed = jax.random.randint(jax.random.fold_in(key, 1), (pairs,), 0, 1 << 20) % (room + 1)
    lengths = lengths.at[1:1 + 2 * pairs:2].set(donor - passed).at[2:2 + 2 * pairs:2].set(taker + passed)
    return lengths[jax.random.permutation(jax.random.fold_in(key, 2), number_of)]


def gaussian(own_key, extent, scale, bound, split=(), held_as=jnp.bfloat16):
    values = scale * jax.random.normal(own_key, extent, jnp.float32)
    if split:
        values = values * steps_of(own_key, extent, split, -0.22, 0.18)
    return jnp.clip(values, -bound, bound).astype(held_as)


def setup_inputs(seed: int = 0) -> dict:
    seeds = jax.random.split(jax.random.key(seed), 17)
    hidden_in = gaussian(seeds[0], (MB, SEQS, SEQ_LEN, D), 1.0, 6.0, ((1, 32),))
    segment_ids = jax.vmap(lambda own: jnp.searchsorted(jnp.cumsum(uneven_parts(own, SEGS, SEQ_LEN, SEG_MOST, 0)), jnp.arange(SEQ_LEN), side="right"))(jax.random.split(seeds[1], MB * SEQS)).reshape((MB, SEQS, SEQ_LEN)).astype(jnp.int32)
    rel_bucket = touch_ends(jax.random.randint(seeds[2], (MB, SEQS, SEQ_LEN, SEQ_LEN), 0, REL_BUCKETS), jax.random.fold_in(seeds[2], 1), 0, REL_BUCKETS - 1).astype(jnp.int32)
    layout_bucket = touch_ends(jax.random.randint(seeds[3], (MB, SEQS, SEQ_LEN, SEQ_LEN), 0, LAYOUT_BUCKETS), jax.random.fold_in(seeds[3], 1), 0, LAYOUT_BUCKETS - 1).astype(jnp.int32)
    w_query = gaussian(seeds[4], (D, INNER), (5 * D) ** -0.5, 0.078125, ((0, 32),))
    w_key = gaussian(seeds[5], (D, INNER), (5 * D) ** -0.5, 0.078125, ((0, 32),))
    w_value = gaussian(seeds[6], (D, INNER), D ** -0.5, 0.1875, ((0, 32),))
    w_out = gaussian(seeds[7], (INNER, D), (INNER // 16) ** -0.5, 0.75, ((0, 32),))
    norm_one = jnp.clip(1.0 + 0.1 * jax.random.normal(seeds[8], (D,), jnp.float32), 0.5, 1.5).astype(jnp.bfloat16)
    rel_table = gaussian(seeds[9], (REL_BUCKETS * HEADS,), 0.5, 3.0, ((0, 32),))
    layout_table = gaussian(seeds[10], (LAYOUT_BUCKETS * HEADS,), 0.5, 3.0, ((0, 32),))
    norm_two = jnp.clip(1.0 + 0.1 * jax.random.normal(seeds[11], (D,), jnp.float32), 0.5, 1.5).astype(jnp.bfloat16)
    w_gate = gaussian(seeds[12], (D, FF), D ** -0.5, 0.1875, ((0, 32),))
    w_up = gaussian(seeds[13], (D, FF), D ** -0.5, 0.1875, ((0, 32),))
    w_down = gaussian(seeds[14], (FF, D), (FF // 2) ** -0.5, 0.15625, ((0, 32),))
    out_grad = gaussian(seeds[15], (MB, SEQS, SEQ_LEN, D), 1.0, 6.0, ((1, 32),))
    return {"hidden_in": hidden_in, "segment_ids": segment_ids, "rel_bucket": rel_bucket, "layout_bucket": layout_bucket, "w_query": w_query, "w_key": w_key, "w_value": w_value, "w_out": w_out, "norm_one": norm_one, "rel_table": rel_table, "layout_table": layout_table, "norm_two": norm_two, "w_gate": w_gate, "w_up": w_up, "w_down": w_down, "out_grad": out_grad}


EPSILON = 1e-06
MASKED = -1e+30
HIGHEST = lax.Precision.HIGHEST

@jax.custom_vjp
def low(v):
    return lax.optimization_barrier(v.astype(jnp.bfloat16)).astype(jnp.float32)

@jax.custom_vjp
def low_back(v):
    return v

def low_keep(v):
    return (low(v), None)

def low_pass(kept, grad):
    return (grad,)

def back_keep(v):
    return (v, None)

def back_low(kept, grad):
    return (low(grad),)
low.defvjp(low_keep, low_pass)
low_back.defvjp(back_keep, back_low)

def gelu_tanh(values):
    return 0.5 * values * (1.0 + jnp.tanh(0.7978845608028654 * (values + 0.044715 * values * values * values)))

def rms_scale(values, gain_vec):
    return values * lax.rsqrt(lax.optimization_barrier(jnp.mean(values * values, axis=-1, keepdims=True)) + EPSILON) * gain_vec

def position_bias(rel_full, lay_full, rel_ids, lay_ids):
    bias = rel_full.reshape(REL_BUCKETS, HEADS)[rel_ids] + lay_full.reshape(LAYOUT_BUCKETS, HEADS)[lay_ids]
    return jnp.transpose(bias, (2, 0, 1))

def one_sequence(weights, sequence):
    w_query, w_key, w_value, w_out, norm_one, rel_table, layout_table, norm_two, w_gate, w_up, w_down = weights
    inputs, segment, rel_ids, lay_ids = sequence
    head_shape = (SEQ_LEN, HEADS, HEAD_DIM)
    normed = low(rms_scale(inputs, norm_one))
    queries = low_back(low(jnp.dot(normed, w_query, precision=HIGHEST))).reshape(head_shape)
    key_heads = low_back(low(jnp.dot(normed, w_key, precision=HIGHEST))).reshape(head_shape)
    value_heads = low_back(low(jnp.dot(normed, w_value, precision=HIGHEST))).reshape(head_shape)
    scores = jnp.einsum('qhd,khd->hqk', queries, key_heads, precision=HIGHEST)
    scores = low_back(scores + position_bias(rel_table, layout_table, rel_ids, lay_ids))
    same_doc = segment[:, None] == segment[None, :]
    scores = jnp.where(same_doc[None], scores, MASKED)
    probs_low = low(jax.nn.softmax(scores, axis=-1))
    attended = jnp.einsum('hqk,khd->qhd', probs_low, value_heads, precision=HIGHEST)
    attended = low_back(low(attended.reshape(SEQ_LEN, HEADS * HEAD_DIM)))
    middle = inputs + low_back(jnp.dot(attended, w_out, precision=HIGHEST))
    normed_two = low(rms_scale(middle, norm_two))
    gate_proj = low_back(jnp.dot(normed_two, w_gate, precision=HIGHEST))
    up_proj = low_back(jnp.dot(normed_two, w_up, precision=HIGHEST))
    hidden = low_back(low(gelu_tanh(gate_proj) * up_proj))
    return middle + low_back(jnp.dot(hidden, w_down, precision=HIGHEST))

def reference(hidden_in, segment_ids, rel_bucket, layout_bucket, w_query, w_key, w_value, w_out, norm_one, rel_table, layout_table, norm_two, w_gate, w_up, w_down, out_grad):
    weights = tuple((weight.astype(jnp.float32) for weight in (w_query, w_key, w_value, w_out, norm_one, rel_table, layout_table, norm_two, w_gate, w_up, w_down)))
    total_rows = hidden_in.shape[0] * hidden_in.shape[1]
    segment_rows = segment_ids.reshape(total_rows, SEQ_LEN)
    rel_rows = rel_bucket.reshape(total_rows, SEQ_LEN, SEQ_LEN)
    lay_rows = layout_bucket.reshape(total_rows, SEQ_LEN, SEQ_LEN)

    def forward(inputs, params):

        def one_step(sequence):
            return one_sequence(params, sequence)
        rows_out = lax.map(jax.checkpoint(one_step), (inputs.reshape(total_rows, SEQ_LEN, D), segment_rows, rel_rows, lay_rows))
        return rows_out.reshape(inputs.shape)
    result, pullback = jax.vjp(forward, hidden_in.astype(jnp.float32), weights)
    grad_input, grads = pullback(out_grad.astype(jnp.float32))
    return (result.astype(jnp.bfloat16), grad_input.astype(jnp.bfloat16), grads[0], grads[1], grads[2], grads[3], grads[4], grads[5], grads[6], grads[7], grads[8], grads[9], grads[10])
```

```python
import functools
import jax, jax.numpy as jnp
from jax import lax
from jax.experimental import pallas as pl
from jax.experimental.pallas import tpu as pltpu
from jax.sharding import PartitionSpec as P

MESH = pl.DeviceIdType.MESH
AXES = ("wide", "narrow")

def place():
    wide = lax.axis_index("wide")
    return wide // 4, (wide // 2) % 2, wide % 2, lax.axis_index("narrow")

def device(z, x, c, y):
    return ((z * 2 + x) * 2 + c, y)

def greet(nz):
    z, x, c, y = place()
    peers = [device(z, x, 1 - c, y), device(z, 1 - x, c, y), device(z, x, c, 1 - y)]
    peers += [device(lax.rem(z + d, nz), x, c, y) for d in range(1, nz)]
    barrier = pltpu.get_barrier_semaphore()
    for peer in peers:
        pl.semaphore_signal(barrier, inc=1, device_id=peer, device_id_type=MESH)
    pl.semaphore_wait(barrier, len(peers))

def split_of(cols):
    half = (cols // 2 + 64) // 128 * 128
    return half

def gather_body(nz, pieces, count, *refs):
    shards, fulls = refs[:count], refs[count:2 * count]
    send, recv, local = refs[2 * count:]
    z, x, c, y = place()
    def remote(src, dst, k, slot, peer):
        return pltpu.make_async_remote_copy(src_ref=src, dst_ref=dst, send_sem=send.at[k, slot],
            recv_sem=recv.at[k, slot], device_id=peer, device_id_type=MESH)
    owns, zs, firsts, seconds, sibs = [], [], [], [], []
    for k, (a, c0, cn) in enumerate(pieces):
        col = pl.ds(c0, cn); h = split_of(cn)
        ca, cb = pl.ds(c0, h), pl.ds(c0 + h, cn - h)
        full = fulls[a]
        own = full.at[z, x, c, y, :, col]
        owns.append(pltpu.make_async_copy(shards[a].at[:, col], own, local.at[k]))
        zs.append([remote(shards[a].at[:, col], own, k, d - 1, device(lax.rem(z + d, nz), x, c, y)) for d in range(1, nz)])
        s = nz - 1
        f = []
        if h: f.append(remote(full.at[:, x, c, y, :, ca], full.at[:, x, c, y, :, ca], k, s, device(z, 1 - x, c, y)))
        if cn > h: f.append(remote(full.at[:, x, c, y, :, cb], full.at[:, x, c, y, :, cb], k, s + 1, device(z, x, c, 1 - y)))
        firsts.append(f)
        f = []
        if h: f.append(remote(full.at[:, :, c, y, :, ca], full.at[:, :, c, y, :, ca], k, s + 2, device(z, x, c, 1 - y)))
        if cn > h: f.append(remote(full.at[:, x, c, :, :, cb], full.at[:, x, c, :, :, cb], k, s + 3, device(z, 1 - x, c, y)))
        seconds.append(f)
        sibs.append([remote(full.at[:, :, c, :, :, col], full.at[:, :, c, :, :, col], k, s + 4, device(z, x, 1 - c, y))])
    n = len(pieces)
    for k in range(n):
        owns[k].start()
    greet(nz)
    for k in range(n):
        for d in zs[k]: d.start()
    for t in range(n + 2):
        if t < n:
            owns[t].wait()
            for d in zs[t]: d.wait_recv()
            for d in firsts[t]: d.start()
        if 0 <= t - 1 < n:
            for d in firsts[t - 1]: d.wait_recv()
            for d in seconds[t - 1]: d.start()
        if 0 <= t - 2 < n:
            for d in seconds[t - 2]: d.wait_recv()
            for d in sibs[t - 2]: d.start()
    for k in range(n):
        for d in sibs[k]: d.wait_recv()
        for d in zs[k] + firsts[k] + seconds[k] + sibs[k]: d.wait_send()

def gather(mesh, shards, pieces, cid):
    nz = mesh.shape["wide"] // 4
    count = len(shards)
    outs = [jax.ShapeDtypeStruct((nz, 2, 2, mesh.shape["narrow"]) + s.shape, s.dtype) for s in shards]
    n = len(pieces); slots = nz - 1 + 5
    return pl.pallas_call(functools.partial(gather_body, nz, pieces, count), out_shape=outs,
        in_specs=[pl.BlockSpec(memory_space=pl.ANY)] * count,
        out_specs=[pl.BlockSpec(memory_space=pl.ANY)] * count,
        scratch_shapes=[pltpu.SemaphoreType.DMA((n, slots)), pltpu.SemaphoreType.DMA((n, slots)), pltpu.SemaphoreType.DMA((n,))],
        compiler_params=pltpu.CompilerParams(collective_id=cid, has_side_effects=True, vmem_limit_bytes=8 << 20))(*shards)

def rows_loop(count, fn):
    lax.fori_loop(0, count, lambda i, _: (fn(i), 0)[1], 0)

def scatter_body(nz, pieces, count, *refs):
    fulls, outs = refs[:count], refs[count:2 * count]
    rest = refs[2 * count:]
    n = len(pieces)
    bufs = rest[:5 * n]
    send, recv, local = rest[5 * n:]
    z, x, c, y = place()
    def remote(src, dst, k, slot, peer):
        return pltpu.make_async_remote_copy(src_ref=src, dst_ref=dst, send_sem=send.at[k, slot],
            recv_sem=recv.at[k, slot], device_id=peer, device_id_type=MESH)
    greet(nz)
    loads, sibs, firsts, seconds, thirds = [], [], [], [], []
    for k, (a, c0, cn) in enumerate(pieces):
        col = pl.ds(c0, cn); h = split_of(cn)
        p0, r0, r1, r2, r3 = bufs[5 * k:5 * k + 5]
        full = fulls[a]
        loads.append(pltpu.make_async_copy(full.at[:, :, c, :, :, col], p0, local.at[k]))
        sibs.append([remote(full.at[:, :, 1 - c, :, :, col], r0, k, 0, device(z, x, 1 - c, y))])
        A, B = pl.ds(0, h), pl.ds(h, cn - h)
        f = []
        if h: f.append(remote(p0.at[:, :, 1 - y, :, A], r1.at[:, :, :, A], k, 1, device(z, x, c, 1 - y)))
        if cn > h: f.append(remote(p0.at[:, 1 - x, :, :, B], r1.at[:, :, :, B], k, 2, device(z, 1 - x, c, y)))
        firsts.append(f)
        f = []
        if h: f.append(remote(p0.at[:, 1 - x, y, :, A], r2.at[:, :, A], k, 3, device(z, 1 - x, c, y)))
        if cn > h: f.append(remote(p0.at[:, x, 1 - y, :, B], r2.at[:, :, B], k, 4, device(z, x, c, 1 - y)))
        seconds.append(f)
        thirds.append([remote(p0.at[lax.rem(z + d, nz), x, y], r3.at[d - 1], k, 4 + d, device(lax.rem(z + d, nz), x, c, y)) for d in range(1, nz)])
    for k in range(n):
        loads[k].start()
        for d in sibs[k]: d.start()
    for t in range(n + 3):
        k = t
        if k < n:
            p0, r0, r1, r2, r3 = bufs[5 * k:5 * k + 5]
            loads[k].wait()
            for d in sibs[k]: d.wait_recv()
            def add0(i, p0=p0, r0=r0):
                i0, i1, i2 = i // 4, (i // 2) % 2, i % 2
                p0[i0, i1, i2] = p0[i0, i1, i2] + r0[i0, i1, i2]
            rows_loop(nz * 4, add0)
            for d in firsts[k]: d.start()
        k = t - 1
        if 0 <= k < n:
            p0, r0, r1, r2, r3 = bufs[5 * k:5 * k + 5]
            cn = pieces[k][2]; h = split_of(cn)
            for d in firsts[k]: d.wait_recv()
            def add1(i, p0=p0, r1=r1, h=h, cn=cn):
                i0, i1 = i // 2, i % 2
                if h: p0[i0, i1, y, :, :h] = p0[i0, i1, y, :, :h] + r1[i0, i1, :, :h]
                if cn > h: p0[i0, x, i1, :, h:] = p0[i0, x, i1, :, h:] + r1[i0, i1, :, h:]
            rows_loop(nz * 2, add1)
            for d in seconds[k]: d.start()
        k = t - 2
        if 0 <= k < n:
            p0, r0, r1, r2, r3 = bufs[5 * k:5 * k + 5]
            for d in seconds[k]: d.wait_recv()
            def add2(i, p0=p0, r2=r2):
                p0[i, x, y] = p0[i, x, y] + r2[i]
            rows_loop(nz, add2)
            for d in thirds[k]: d.start()
        k = t - 3
        if 0 <= k < n:
            p0, r0, r1, r2, r3 = bufs[5 * k:5 * k + 5]
            a, c0, cn = pieces[k]
            for d in thirds[k]: d.wait_recv()
            total = p0[z, x, y].astype(jnp.float32)
            for d in range(1, nz):
                total = total + r3[d - 1].astype(jnp.float32)
            outs[a][:, c0:c0 + cn] = total
    for k in range(n):
        for d in sibs[k] + firsts[k] + seconds[k] + thirds[k]: d.wait_send()

def scatter(mesh, fulls, pieces, cid):
    nz = mesh.shape["wide"] // 4
    count = len(fulls)
    outs = [jax.ShapeDtypeStruct(s.shape[4:], jnp.float32) for s in fulls]
    n = len(pieces); slots = 4 + nz
    scratch = []
    for a, c0, cn in pieces:
        r = fulls[a].shape[4]
        dt = fulls[a].dtype
        scratch += [pltpu.VMEM((nz, 2, 2, r, cn), dt), pltpu.VMEM((nz, 2, 2, r, cn), dt), pltpu.VMEM((nz, 2, r, cn), dt), pltpu.VMEM((nz, r, cn), dt), pltpu.VMEM((nz - 1, r, cn), dt)]
    return pl.pallas_call(functools.partial(scatter_body, nz, pieces, count), out_shape=outs,
        in_specs=[pl.BlockSpec(memory_space=pl.ANY)] * count,
        out_specs=[pl.BlockSpec(memory_space=pltpu.VMEM)] * count,
        scratch_shapes=scratch + [pltpu.SemaphoreType.DMA((n, slots)), pltpu.SemaphoreType.DMA((n, slots)), pltpu.SemaphoreType.DMA((n,))],
        compiler_params=pltpu.CompilerParams(collective_id=cid, has_side_effects=True, vmem_limit_bytes=60 << 20))(*fulls)


HEADS = 16
HEAD_DIM = 64
REL_BUCKETS = 32
LAYOUT_BUCKETS = 64
EPSILON = 1e-06
MASKED = -1e30
SMALL_ROWS = 8
SMALL_COLS = 128


def gelu_tanh(values):
    return (
        0.5
        * values
        * (1.0 + jnp.tanh(0.7978845608028654 * (values + 0.044715 * values * values * values)))
    )


def rms_scale(values, gain_vec):
    return (
        values * lax.rsqrt(jnp.mean(values * values, axis=-1, keepdims=True) + EPSILON) * gain_vec
    )


def matmul(first, second, dims):
    return lax.dot_general(first, second, (dims, ((), ())), preferred_element_type=jnp.float32)


NN = ((1,), (0,))
NT = ((1,), (1,))
TN = ((0,), (0,))


def one_hots(rel_row, lay_row):
    rel_hot = jnp.arange(REL_BUCKETS)[:, None] == rel_row.reshape(1, -1)
    lay_hot = jnp.arange(LAYOUT_BUCKETS)[:, None] == lay_row.reshape(1, -1)
    return jnp.concatenate([rel_hot, lay_hot], axis=0).astype(jnp.bfloat16)


def attention(queries, key_heads, value_heads, segment, rel_row, lay_row, tables):
    length = queries.shape[0]
    hots = one_hots(rel_row, lay_row)
    bias = matmul(tables, hots, TN).reshape(HEADS, length, length)
    scores = jnp.einsum("qhd,khd->hqk", queries, key_heads, preferred_element_type=jnp.float32)
    same_doc = segment[:, None] == segment[None, :]
    scores = jnp.where(same_doc[None], scores + bias, MASKED)
    shifted = jnp.exp(scores - jnp.max(scores, axis=-1, keepdims=True))
    probs = shifted / jnp.sum(shifted, axis=-1, keepdims=True)
    attended = jnp.einsum(
        "hqk,khd->qhd", probs.astype(jnp.bfloat16), value_heads, preferred_element_type=jnp.float32
    )
    return attended.astype(jnp.bfloat16), probs, hots


def attention_back(queries, key_heads, value_heads, probs, hots, grad_attended):
    grad_value = jnp.einsum(
        "hqk,qhd->khd", probs.astype(jnp.bfloat16), grad_attended, preferred_element_type=jnp.float32
    )
    grad_prob = jnp.einsum(
        "qhd,khd->hqk", grad_attended, value_heads, preferred_element_type=jnp.float32
    )
    grad_score = (
        probs * (grad_prob - jnp.sum(grad_prob * probs, axis=-1, keepdims=True))
    ).astype(jnp.bfloat16)
    grad_query = jnp.einsum(
        "hqk,khd->qhd", grad_score, key_heads, preferred_element_type=jnp.float32
    )
    grad_key = jnp.einsum(
        "hqk,qhd->khd", grad_score, queries, preferred_element_type=jnp.float32
    )
    grad_tables = matmul(hots, grad_score.reshape(HEADS, -1), NT)
    return (
        grad_query.astype(jnp.bfloat16),
        grad_key.astype(jnp.bfloat16),
        grad_value.astype(jnp.bfloat16),
        grad_tables,
    )


def pack_small(vectors, grid):
    packed = jnp.concatenate([v.reshape(grid + (-1,)) for v in vectors], axis=-1)
    spare = SMALL_COLS - packed.shape[-1]
    packed = jnp.pad(packed, ((0, 0),) * len(grid) + ((0, spare),))
    return jnp.broadcast_to(packed[..., None, :], grid + (SMALL_ROWS, SMALL_COLS))


def unpack_small(block, sizes):
    out, at = [], 0
    for size in sizes:
        out.append(block[..., 0, at : at + size].reshape(-1))
        at += size
    return out


def column_pieces(index, cols, parts):
    step = cols // parts // 128 * 128
    edges = [step * i for i in range(parts)] + [cols]
    return [(index, edges[i], edges[i + 1] - edges[i]) for i in range(parts)]


def shards(mesh, *args):
    (hidden_in, segment_ids, rel_bucket, layout_bucket, w_query, w_key, w_value, w_out) = args[:8]
    (norm_one, rel_table, layout_table, norm_two, w_gate, w_up, w_down, out_grad) = args[8:]
    grid = (mesh.shape["wide"] // 4, 2, 2, mesh.shape["narrow"])
    micro, rows, length, features = hidden_in.shape
    tokens = micro * rows * length
    sizes = [v.shape[0] for v in (norm_one, rel_table, layout_table, norm_two)]
    small = pack_small((norm_one, rel_table, layout_table, norm_two), ())
    parts = (small, w_query, w_key, w_value, w_out, w_gate, w_up, w_down)
    pieces = []
    for index, part in enumerate(parts):
        pieces += column_pieces(index, part.shape[1], 2 if index > 4 else 1)
    fulls = gather(mesh, parts, pieces, 1)
    gain_one, rel_full, lay_full, gain_two = unpack_small(fulls[0], sizes)
    gain_one, gain_two = gain_one.astype(jnp.float32), gain_two.astype(jnp.float32)
    wq, wk, wv, wo, wg, wu, wd = [f.reshape(-1, f.shape[-1]) for f in fulls[1:]]
    tables = jnp.concatenate([rel_full.reshape(-1, HEADS), lay_full.reshape(-1, HEADS)], axis=0)

    flat = hidden_in.reshape(tokens, features).astype(jnp.float32)
    normed, back_one = jax.vjp(rms_scale, flat, gain_one)
    normed = normed.astype(jnp.bfloat16)
    head_shape = (micro * rows, length, HEADS, HEAD_DIM)
    queries, keys, values = [
        matmul(normed, w, NN).astype(jnp.bfloat16).reshape(head_shape) for w in (wq, wk, wv)
    ]
    seg = segment_ids.reshape(-1, length)
    rel = rel_bucket.reshape(-1, length, length)
    lay = layout_bucket.reshape(-1, length, length)
    kept = [
        attention(queries[i], keys[i], values[i], seg[i], rel[i], lay[i], tables)
        for i in range(micro * rows)
    ]
    attended = jnp.concatenate([k[0].reshape(length, -1) for k in kept], axis=0)
    middle = flat + matmul(attended, wo, NN)
    normed_two, back_two = jax.vjp(rms_scale, middle, gain_two)
    normed_two = normed_two.astype(jnp.bfloat16)
    gate = matmul(normed_two, wg, NN)
    up = matmul(normed_two, wu, NN)
    gelu_value, gelu_back = jax.vjp(gelu_tanh, gate)
    hidden = (gelu_value * up).astype(jnp.bfloat16)
    output = (middle + matmul(hidden, wd, NN)).astype(jnp.bfloat16)

    dy = out_grad.reshape(tokens, features)
    grad_down = matmul(hidden, dy, TN)
    d_hidden = matmul(dy, wd, NT).astype(jnp.bfloat16).astype(jnp.float32)
    d_gate = gelu_back(d_hidden * up)[0].astype(jnp.bfloat16)
    d_up = (d_hidden * gelu_value).astype(jnp.bfloat16)
    grad_gate = matmul(normed_two, d_gate, TN)
    grad_up = matmul(normed_two, d_up, TN)
    d_normed_two = matmul(d_gate, wg, NT) + matmul(d_up, wu, NT)
    middle_part, grad_gain_two = back_two(d_normed_two)
    d_middle = dy.astype(jnp.float32) + middle_part
    d_branch = d_middle.astype(jnp.bfloat16)
    grad_out = matmul(attended, d_branch, TN)
    d_attended = matmul(d_branch, wo, NT).astype(jnp.bfloat16).reshape(head_shape)
    backs = [
        attention_back(queries[i], keys[i], values[i], kept[i][1], kept[i][2], d_attended[i])
        for i in range(micro * rows)
    ]
    d_query, d_key, d_value = [
        jnp.concatenate([b[j].reshape(length, -1) for b in backs], axis=0) for j in range(3)
    ]
    grad_tables = sum(b[3] for b in backs)
    grad_query = matmul(normed, d_query, TN)
    grad_key = matmul(normed, d_key, TN)
    grad_value = matmul(normed, d_value, TN)
    d_normed = matmul(d_query, wq, NT) + matmul(d_key, wk, NT) + matmul(d_value, wv, NT)
    input_part, grad_gain_one = back_one(d_normed)
    in_grad = (d_middle + input_part).astype(jnp.bfloat16)

    grads = [
        g.astype(jnp.bfloat16).reshape(grid + p.shape)
        for g, p in zip(
            (grad_query, grad_key, grad_value, grad_out, grad_gate, grad_up, grad_down), parts[1:]
        )
    ]
    small_grads = pack_small(
        (
            grad_gain_one,
            grad_tables[:REL_BUCKETS].reshape(-1),
            grad_tables[REL_BUCKETS:].reshape(-1),
            grad_gain_two,
        ),
        grid,
    )
    order = [7, 5, 6, 4, 1, 2, 3, 0]
    out_pieces = [p for index in order for p in pieces if p[0] == index]
    small_sum, *sums = scatter(mesh, [small_grads] + grads, out_pieces, 2)
    g_one, g_rel, g_lay, g_two = unpack_small(small_sum, sizes)
    shape = hidden_in.shape
    return (
        output.reshape(shape),
        in_grad.reshape(shape),
        *sums[:4],
        g_one,
        g_rel,
        g_lay,
        g_two,
        *sums[4:],
    )


def solution(mesh):
    both = ("wide", "narrow")
    tokens4 = P(None, both, None, None)
    weight = P(both, None)
    vector = P(both)
    return jax.shard_map(
        functools.partial(shards, mesh),
        mesh=mesh,
        in_specs=(
            tokens4,
            P(None, both, None),
            tokens4,
            tokens4,
            weight,
            weight,
            weight,
            weight,
            vector,
            vector,
            vector,
            vector,
            weight,
            weight,
            weight,
            tokens4,
        ),
        out_specs=(
            tokens4,
            tokens4,
            weight,
            weight,
            weight,
            weight,
            vector,
            vector,
            vector,
            vector,
            weight,
            weight,
            weight,
        ),
        check_vma=False,
    )
```

```python
import functools
import jax, jax.numpy as jnp
from jax import lax
from jax.experimental import pallas as pl
from jax.experimental.pallas import tpu as pltpu
from jax.sharding import PartitionSpec as P

MESH = pl.DeviceIdType.MESH
AXES = ("wide", "narrow")

def place():
    wide = lax.axis_index("wide")
    return wide // 4, (wide // 2) % 2, wide % 2, lax.axis_index("narrow")

def device(z, x, c, y):
    return ((z * 2 + x) * 2 + c, y)

def greet(nz):
    z, x, c, y = place()
    peers = [device(z, x, 1 - c, y), device(z, 1 - x, c, y), device(z, x, c, 1 - y)]
    peers += [device(lax.rem(z + d, nz), x, c, y) for d in range(1, nz)]
    barrier = pltpu.get_barrier_semaphore()
    for peer in peers:
        pl.semaphore_signal(barrier, inc=1, device_id=peer, device_id_type=MESH)
    pl.semaphore_wait(barrier, len(peers))

def split_of(cols):
    half = (cols // 2 + 64) // 128 * 128
    return half

def gather_body(nz, pieces, count, *refs):
    shards, fulls = refs[:count], refs[count:2 * count]
    send, recv, local = refs[2 * count:]
    z, x, c, y = place()
    def remote(src, dst, k, slot, peer):
        return pltpu.make_async_remote_copy(src_ref=src, dst_ref=dst, send_sem=send.at[k, slot],
            recv_sem=recv.at[k, slot], device_id=peer, device_id_type=MESH)
    owns, zs, firsts, seconds, sibs = [], [], [], [], []
    for k, (a, c0, cn) in enumerate(pieces):
        col = pl.ds(c0, cn); h = split_of(cn)
        ca, cb = pl.ds(c0, h), pl.ds(c0 + h, cn - h)
        full = fulls[a]
        own = full.at[z, x, c, y, :, col]
        owns.append(pltpu.make_async_copy(shards[a].at[:, col], own, local.at[k]))
        zs.append([remote(shards[a].at[:, col], own, k, d - 1, device(lax.rem(z + d, nz), x, c, y)) for d in range(1, nz)])
        s = nz - 1
        f = []
        if h: f.append(remote(full.at[:, x, c, y, :, ca], full.at[:, x, c, y, :, ca], k, s, device(z, 1 - x, c, y)))
        if cn > h: f.append(remote(full.at[:, x, c, y, :, cb], full.at[:, x, c, y, :, cb], k, s + 1, device(z, x, c, 1 - y)))
        firsts.append(f)
        f = []
        if h: f.append(remote(full.at[:, :, c, y, :, ca], full.at[:, :, c, y, :, ca], k, s + 2, device(z, x, c, 1 - y)))
        if cn > h: f.append(remote(full.at[:, x, c, :, :, cb], full.at[:, x, c, :, :, cb], k, s + 3, device(z, 1 - x, c, y)))
        seconds.append(f)
        sibs.append([remote(full.at[:, :, c, :, :, col], full.at[:, :, c, :, :, col], k, s + 4, device(z, x, 1 - c, y))])
    n = len(pieces)
    for k in range(n):
        owns[k].start()
    greet(nz)
    for k in range(n):
        for d in zs[k]: d.start()
    for t in range(n + 2):
        if t < n:
            owns[t].wait()
            for d in zs[t]: d.wait_recv()
            for d in firsts[t]: d.start()
        if 0 <= t - 1 < n:
            for d in firsts[t - 1]: d.wait_recv()
            for d in seconds[t - 1]: d.start()
        if 0 <= t - 2 < n:
            for d in seconds[t - 2]: d.wait_recv()
            for d in sibs[t - 2]: d.start()
    for k in range(n):
        for d in sibs[k]: d.wait_recv()
        for d in zs[k] + firsts[k] + seconds[k] + sibs[k]: d.wait_send()

def gather(mesh, shards, pieces, cid):
    nz = mesh.shape["wide"] // 4
    count = len(shards)
    outs = [jax.ShapeDtypeStruct((nz, 2, 2, mesh.shape["narrow"]) + s.shape, s.dtype) for s in shards]
    n = len(pieces); slots = nz - 1 + 5
    return pl.pallas_call(functools.partial(gather_body, nz, pieces, count), out_shape=outs,
        in_specs=[pl.BlockSpec(memory_space=pl.ANY)] * count,
        out_specs=[pl.BlockSpec(memory_space=pl.ANY)] * count,
        scratch_shapes=[pltpu.SemaphoreType.DMA((n, slots)), pltpu.SemaphoreType.DMA((n, slots)), pltpu.SemaphoreType.DMA((n,))],
        compiler_params=pltpu.CompilerParams(collective_id=cid, has_side_effects=True, vmem_limit_bytes=8 << 20))(*shards)

def rows_loop(count, fn):
    lax.fori_loop(0, count, lambda i, _: (fn(i), 0)[1], 0)

def scatter_body(nz, pieces, count, *refs):
    fulls, outs = refs[:count], refs[count:2 * count]
    rest = refs[2 * count:]
    n = len(pieces)
    bufs = rest[:5 * n]
    send, recv, local = rest[5 * n:]
    z, x, c, y = place()
    def remote(src, dst, k, slot, peer):
        return pltpu.make_async_remote_copy(src_ref=src, dst_ref=dst, send_sem=send.at[k, slot],
            recv_sem=recv.at[k, slot], device_id=peer, device_id_type=MESH)
    greet(nz)
    loads, sibs, firsts, seconds, thirds = [], [], [], [], []
    for k, (a, c0, cn) in enumerate(pieces):
        col = pl.ds(c0, cn); h = split_of(cn)
        p0, r0, r1, r2, r3 = bufs[5 * k:5 * k + 5]
        full = fulls[a]
        loads.append(pltpu.make_async_copy(full.at[:, :, c, :, :, col], p0, local.at[k]))
        sibs.append([remote(full.at[:, :, 1 - c, :, :, col], r0, k, 0, device(z, x, 1 - c, y))])
        A, B = pl.ds(0, h), pl.ds(h, cn - h)
        f = []
        if h: f.append(remote(p0.at[:, :, 1 - y, :, A], r1.at[:, :, :, A], k, 1, device(z, x, c, 1 - y)))
        if cn > h: f.append(remote(p0.at[:, 1 - x, :, :, B], r1.at[:, :, :, B], k, 2, device(z, 1 - x, c, y)))
        firsts.append(f)
        f = []
        if h: f.append(remote(p0.at[:, 1 - x, y, :, A], r2.at[:, :, A], k, 3, device(z, 1 - x, c, y)))
        if cn > h: f.append(remote(p0.at[:, x, 1 - y, :, B], r2.at[:, :, B], k, 4, device(z, x, c, 1 - y)))
        seconds.append(f)
        thirds.append([remote(p0.at[lax.rem(z + d, nz), x, y], r3.at[d - 1], k, 4 + d, device(lax.rem(z + d, nz), x, c, y)) for d in range(1, nz)])
    for k in range(n):
        loads[k].start()
        for d in sibs[k]: d.start()
    for t in range(n + 3):
        k = t
        if k < n:
            p0, r0, r1, r2, r3 = bufs[5 * k:5 * k + 5]
            loads[k].wait()
            for d in sibs[k]: d.wait_recv()
            def add0(i, p0=p0, r0=r0):
                i0, i1, i2 = i // 4, (i // 2) % 2, i % 2
                p0[i0, i1, i2] = p0[i0, i1, i2] + r0[i0, i1, i2]
            rows_loop(nz * 4, add0)
            for d in firsts[k]: d.start()
        k = t - 1
        if 0 <= k < n:
            p0, r0, r1, r2, r3 = bufs[5 * k:5 * k + 5]
            cn = pieces[k][2]; h = split_of(cn)
            for d in firsts[k]: d.wait_recv()
            def add1(i, p0=p0, r1=r1, h=h, cn=cn):
                i0, i1 = i // 2, i % 2
                if h: p0[i0, i1, y, :, :h] = p0[i0, i1, y, :, :h] + r1[i0, i1, :, :h]
                if cn > h: p0[i0, x, i1, :, h:] = p0[i0, x, i1, :, h:] + r1[i0, i1, :, h:]
            rows_loop(nz * 2, add1)
            for d in seconds[k]: d.start()
        k = t - 2
        if 0 <= k < n:
            p0, r0, r1, r2, r3 = bufs[5 * k:5 * k + 5]
            for d in seconds[k]: d.wait_recv()
            def add2(i, p0=p0, r2=r2):
                p0[i, x, y] = p0[i, x, y] + r2[i]
            rows_loop(nz, add2)
            for d in thirds[k]: d.start()
        k = t - 3
        if 0 <= k < n:
            p0, r0, r1, r2, r3 = bufs[5 * k:5 * k + 5]
            a, c0, cn = pieces[k]
            for d in thirds[k]: d.wait_recv()
            total = p0[z, x, y].astype(jnp.float32)
            for d in range(1, nz):
                total = total + r3[d - 1].astype(jnp.float32)
            outs[a][:, c0:c0 + cn] = total
    for k in range(n):
        for d in sibs[k] + firsts[k] + seconds[k] + thirds[k]: d.wait_send()

def scatter(mesh, fulls, pieces, cid):
    nz = mesh.shape["wide"] // 4
    count = len(fulls)
    outs = [jax.ShapeDtypeStruct(s.shape[4:], jnp.float32) for s in fulls]
    n = len(pieces); slots = 4 + nz
    scratch = []
    for a, c0, cn in pieces:
        r = fulls[a].shape[4]
        dt = fulls[a].dtype
        scratch += [pltpu.VMEM((nz, 2, 2, r, cn), dt), pltpu.VMEM((nz, 2, 2, r, cn), dt), pltpu.VMEM((nz, 2, r, cn), dt), pltpu.VMEM((nz, r, cn), dt), pltpu.VMEM((nz - 1, r, cn), dt)]
    return pl.pallas_call(functools.partial(scatter_body, nz, pieces, count), out_shape=outs,
        in_specs=[pl.BlockSpec(memory_space=pl.ANY)] * count,
        out_specs=[pl.BlockSpec(memory_space=pltpu.VMEM)] * count,
        scratch_shapes=scratch + [pltpu.SemaphoreType.DMA((n, slots)), pltpu.SemaphoreType.DMA((n, slots)), pltpu.SemaphoreType.DMA((n,))],
        compiler_params=pltpu.CompilerParams(collective_id=cid, has_side_effects=True, vmem_limit_bytes=60 << 20))(*fulls)


HEADS=16
def dg(a,b,dims): return lax.dot_general(a,b,(dims,((),())),preferred_element_type=jnp.float32)
NN=((1,),(0,)); NT=((1,),(1,)); TN=((0,),(0,))
MASKED=-1e30
def lookup(table_row, ids):
    n,m=ids.shape
    t=jnp.broadcast_to(table_row,(n,128))
    return jnp.concatenate([jnp.take_along_axis(t, ids[:, j:j+128], axis=1) for j in range(0,m,128)],axis=1)
def fwd_body(mode, q_ref,k_ref,v_ref,segc_ref,segr_ref,rel_ref,lay_ref,tab_ref,o_ref,p_ref,bias_ref):
    length=q_ref.shape[0]
    pair=pl.program_id(1)
    lane=lax.broadcasted_iota(jnp.int32,(length,128),1)
    same=segc_ref[0][:, :1]==segr_ref[0]
    q=q_ref[...]; k=k_ref[...]; v=v_ref[...]
    outs=[]
    for h in range(2):
        mine=(lane//64)==h
        qh=jnp.where(mine,q,jnp.zeros_like(q))
        s=dg(qh,k,NT)
        if mode=="gather":
            row=tab_ref[pl.ds(pair*2+h,1),:]
            s=s+(lookup(row,rel_ref[0])+lookup(row,lay_ref[0]+32))
        s=jnp.where(same,s,MASKED)
        e=jnp.exp(s-jnp.max(s,axis=1,keepdims=True))
        p=e/jnp.sum(e,axis=1,keepdims=True)
        p_ref[0,h]=p
        outs.append(dg(p.astype(jnp.bfloat16),v,NN))
    o_ref[...]=jnp.where(lane<64,outs[0],outs[1]).astype(jnp.bfloat16)
def fwd(mode,q,k,v,seg,rel,lay,tab):
    rows,length=seg.shape
    segc=jnp.broadcast_to(seg[:,:,None],(rows,length,128)); segr=jnp.broadcast_to(seg[:,None,:],(rows,8,length))[:, :1]
    blk=pl.BlockSpec((length,128),lambda r,p:(r,p))
    return pl.pallas_call(functools.partial(fwd_body,mode),grid=(rows,HEADS//2),
       in_specs=[blk,blk,blk,pl.BlockSpec((1,length,128),lambda r,p:(r,0,0)),pl.BlockSpec((1,1,length),lambda r,p:(r,0,0)),
         pl.BlockSpec((1,length,length),lambda r,p:(r,0,0)),pl.BlockSpec((1,length,length),lambda r,p:(r,0,0)),pl.BlockSpec((HEADS,128),lambda r,p:(0,0))],
       out_specs=[blk,pl.BlockSpec((1,2,length,length),lambda r,p:(r,p,0,0))],
       out_shape=[jax.ShapeDtypeStruct(q.shape,jnp.bfloat16),jax.ShapeDtypeStruct((rows,HEADS,length,length),jnp.float32)],
       scratch_shapes=[pltpu.VMEM((length,length),jnp.float32)],
       compiler_params=pltpu.CompilerParams(vmem_limit_bytes=32<<20))(q,k,v,segc,segr,rel,lay,tab)

def bwd_body(q_ref,k_ref,v_ref,do_ref,p_ref,dq_ref,dk_ref,dv_ref,ds_ref):
    length=q_ref.shape[0]
    lane=lax.broadcasted_iota(jnp.int32,(length,128),1)
    q=q_ref[...]; k=k_ref[...]; v=v_ref[...]; do=do_ref[...]
    acc=[]
    for h in range(2):
        mine=(lane//64)==h
        doh=jnp.where(mine,do,jnp.zeros_like(do))
        p=p_ref[0,h]
        dp=dg(doh,v,NT)
        ds=(p*(dp-jnp.sum(dp*p,axis=1,keepdims=True))).astype(jnp.bfloat16)
        ds_ref[0,h]=ds
        acc.append((dg(ds,k,NN),dg(ds,q,TN),dg(p.astype(jnp.bfloat16),do,TN)))
    for ref,i in ((dq_ref,0),(dk_ref,1),(dv_ref,2)):
        ref[...]=jnp.where(lane<64,acc[0][i],acc[1][i]).astype(jnp.bfloat16)
def bwd(q,k,v,do,p):
    rows,_,length,_=p.shape
    blk=pl.BlockSpec((length,128),lambda r,p:(r,p))
    big=pl.BlockSpec((1,2,length,length),lambda r,p:(r,p,0,0))
    o=jax.ShapeDtypeStruct(q.shape,jnp.bfloat16)
    return pl.pallas_call(bwd_body,grid=(rows,HEADS//2),in_specs=[blk]*4+[big],out_specs=[blk]*3+[big],
       out_shape=[o,o,o,jax.ShapeDtypeStruct(p.shape,jnp.bfloat16)],compiler_params=pltpu.CompilerParams(vmem_limit_bytes=32<<20))(q,k,v,do,p)

def tab_body(mode,ds_ref,rel_ref,lay_ref,out_ref,t_ref):
    @pl.when(pl.program_id(0)==0)
    def _(): out_ref[...]=jnp.zeros_like(out_ref)
    length=ds_ref.shape[2]
    step=8
    sub=lax.broadcasted_iota(jnp.int32,(32,length),0)
    sub2=lax.broadcasted_iota(jnp.int32,(96,length),0)
    def go(i,_):
        i0=pl.multiple_of(i*step,step)
        rel=rel_ref[0,pl.ds(i0,step),:]; lay=lay_ref[0,pl.ds(i0,step),:]
        if mode=="strided":
            blk=ds_ref[0,:,pl.ds(i0,step),:]
            blk=pltpu.einshape("hid->ihd",blk.astype(jnp.float32)).astype(jnp.bfloat16)
        acc=jnp.zeros((16,128),jnp.float32)
        for j in range(step):
            hot=jnp.concatenate([(sub==rel[j:j+1,:]),(sub2==lay[j:j+1,:])],axis=0).astype(jnp.float32).astype(jnp.bfloat16)
            acc=acc+dg(blk[j],hot,NT)
        out_ref[...]+=acc
        return 0
    lax.fori_loop(0,length//step,go,0)
def tabs(mode,ds,rel,lay):
    rows,_,length,_=ds.shape
    return pl.pallas_call(functools.partial(tab_body,mode),grid=(rows,),in_specs=[pl.BlockSpec((1,16,length,length),lambda r:(r,0,0,0))]+[pl.BlockSpec((1,length,length),lambda r:(r,0,0))]*2,
       out_specs=pl.BlockSpec((16,128),lambda r:(0,0)),out_shape=jax.ShapeDtypeStruct((16,128),jnp.float32),scratch_shapes=[pltpu.VMEM((8,16,length),jnp.bfloat16)],
       compiler_params=pltpu.CompilerParams(vmem_limit_bytes=32<<20))(ds,rel,lay)


REL_BUCKETS = 32
LAYOUT_BUCKETS = 64
EPSILON = 1e-06
SMALL_ROWS = 8
SMALL_COLS = 128


def gelu_tanh(values):
    return (
        0.5
        * values
        * (1.0 + jnp.tanh(0.7978845608028654 * (values + 0.044715 * values * values * values)))
    )


def rms_scale(values, gain_vec):
    return (
        values * lax.rsqrt(jnp.mean(values * values, axis=-1, keepdims=True) + EPSILON) * gain_vec
    )


def matmul(first, second, dims):
    return lax.dot_general(first, second, (dims, ((), ())), preferred_element_type=jnp.float32)


def pack_small(vectors, grid):
    packed = jnp.concatenate([v.reshape(grid + (-1,)) for v in vectors], axis=-1)
    spare = SMALL_COLS - packed.shape[-1]
    packed = jnp.pad(packed, ((0, 0),) * len(grid) + ((0, spare),))
    return jnp.broadcast_to(packed[..., None, :], grid + (SMALL_ROWS, SMALL_COLS))


def unpack_small(block, sizes):
    out, at = [], 0
    for size in sizes:
        out.append(block[..., 0, at : at + size].reshape(-1))
        at += size
    return out


def column_pieces(index, cols, parts):
    step = cols // parts // 128 * 128
    edges = [step * i for i in range(parts)] + [cols]
    return [(index, edges[i], edges[i + 1] - edges[i]) for i in range(parts)]


def shards(mesh, *args):
    (hidden_in, segment_ids, rel_bucket, layout_bucket, w_query, w_key, w_value, w_out) = args[:8]
    (norm_one, rel_table, layout_table, norm_two, w_gate, w_up, w_down, out_grad) = args[8:]
    grid = (mesh.shape["wide"] // 4, 2, 2, mesh.shape["narrow"])
    micro, rows, length, features = hidden_in.shape
    tokens = micro * rows * length
    sizes = [v.shape[0] for v in (norm_one, rel_table, layout_table, norm_two)]
    small = pack_small((norm_one, rel_table, layout_table, norm_two), ())
    parts = (small, w_query, w_key, w_value, w_out, w_gate, w_up, w_down)
    pieces = []
    for index, part in enumerate(parts):
        pieces += column_pieces(index, part.shape[1], 2 if index > 4 else 1)
    fulls = gather(mesh, parts, pieces, 1)
    gain_one, rel_full, lay_full, gain_two = unpack_small(fulls[0], sizes)
    gain_one, gain_two = gain_one.astype(jnp.float32), gain_two.astype(jnp.float32)
    wq, wk, wv, wo, wg, wu, wd = [f.reshape(-1, f.shape[-1]) for f in fulls[1:]]
    tables = jnp.concatenate([rel_full.reshape(-1, HEADS), lay_full.reshape(-1, HEADS)], axis=0)

    flat = hidden_in.reshape(tokens, features).astype(jnp.float32)
    normed, back_one = jax.vjp(rms_scale, flat, gain_one)
    normed = normed.astype(jnp.bfloat16)
    queries, keys, values = [matmul(normed, w, NN).astype(jnp.bfloat16) for w in (wq, wk, wv)]
    seg = segment_ids.reshape(-1, length)
    rel = rel_bucket.reshape(-1, length, length)
    lay = layout_bucket.reshape(-1, length, length)
    table = jnp.pad(jnp.transpose(tables.astype(jnp.float32)), ((0, 0), (0, 128 - tables.shape[0])))
    attended, probs = fwd("gather", queries, keys, values, seg, rel, lay, table)
    middle = flat + matmul(attended, wo, NN)
    normed_two, back_two = jax.vjp(rms_scale, middle, gain_two)
    normed_two = normed_two.astype(jnp.bfloat16)
    gate = matmul(normed_two, wg, NN)
    up = matmul(normed_two, wu, NN)
    gelu_value, gelu_back = jax.vjp(gelu_tanh, gate)
    hidden = (gelu_value * up).astype(jnp.bfloat16)
    output = (middle + matmul(hidden, wd, NN)).astype(jnp.bfloat16)

    dy = out_grad.reshape(tokens, features)
    grad_down = matmul(hidden, dy, TN)
    d_hidden = matmul(dy, wd, NT).astype(jnp.bfloat16).astype(jnp.float32)
    d_gate = gelu_back(d_hidden * up)[0].astype(jnp.bfloat16)
    d_up = (d_hidden * gelu_value).astype(jnp.bfloat16)
    grad_gate = matmul(normed_two, d_gate, TN)
    grad_up = matmul(normed_two, d_up, TN)
    d_normed_two = matmul(d_gate, wg, NT) + matmul(d_up, wu, NT)
    middle_part, grad_gain_two = back_two(d_normed_two)
    d_middle = dy.astype(jnp.float32) + middle_part
    d_branch = d_middle.astype(jnp.bfloat16)
    grad_out = matmul(attended, d_branch, TN)
    d_attended = matmul(d_branch, wo, NT).astype(jnp.bfloat16)
    d_query, d_key, d_value, d_scores = bwd(queries, keys, values, d_attended, probs)
    grad_tables = jnp.transpose(tabs("strided", d_scores, rel, lay))
    grad_query = matmul(normed, d_query, TN)
    grad_key = matmul(normed, d_key, TN)
    grad_value = matmul(normed, d_value, TN)
    d_normed = matmul(d_query, wq, NT) + matmul(d_key, wk, NT) + matmul(d_value, wv, NT)
    input_part, grad_gain_one = back_one(d_normed)
    in_grad = (d_middle + input_part).astype(jnp.bfloat16)

    grads = [
        g.astype(jnp.bfloat16).reshape(grid + p.shape)
        for g, p in zip(
            (grad_query, grad_key, grad_value, grad_out, grad_gate, grad_up, grad_down), parts[1:]
        )
    ]
    small_grads = pack_small(
        (
            grad_gain_one,
            grad_tables[:REL_BUCKETS].reshape(-1),
            grad_tables[REL_BUCKETS : REL_BUCKETS + LAYOUT_BUCKETS].reshape(-1),
            grad_gain_two,
        ),
        grid,
    )
    order = [7, 5, 6, 4, 1, 2, 3, 0]
    out_pieces = [p for index in order for p in pieces if p[0] == index]
    small_sum, *sums = scatter(mesh, [small_grads] + grads, out_pieces, 2)
    g_one, g_rel, g_lay, g_two = unpack_small(small_sum, sizes)
    shape = hidden_in.shape
    return (
        output.reshape(shape),
        in_grad.reshape(shape),
        *sums[:4],
        g_one,
        g_rel,
        g_lay,
        g_two,
        *sums[4:],
    )


def solution(mesh):
    both = ("wide", "narrow")
    tokens4 = P(None, both, None, None)
    weight = P(both, None)
    vector = P(both)
    return jax.shard_map(
        functools.partial(shards, mesh),
        mesh=mesh,
        in_specs=(
            tokens4,
            P(None, both, None),
            tokens4,
            tokens4,
            weight,
            weight,
            weight,
            weight,
            vector,
            vector,
            vector,
            vector,
            weight,
            weight,
            weight,
            tokens4,
        ),
        out_specs=(
            tokens4,
            tokens4,
            weight,
            weight,
            weight,
            weight,
            vector,
            vector,
            vector,
            vector,
            weight,
            weight,
            weight,
        ),
        check_vma=False,
    )
```
